32 devices in a mesh: groups: 2 (over x), tok: 8 (over z, y), head: 2 (over core).
Axes of the slice: x: 2, y: 2, z: 4, core: 2. Of those that a mesh axis runs over, the one named last changes fastest.
Arguments:
- video_query: bfloat16 [2, 4096, 4096], P('groups', ('tok', 'head')), parts along dimension 0, may hold values from -640 to 640
- video_key: bfloat16 [2, 4096, 4096], P('groups', ('tok', 'head')), parts along dimension 0, may hold values from -6 to 6
- video_value: bfloat16 [2, 4096, 4096], P('groups', ('tok', 'head')), parts along dimension 0, may hold values from -6 to 6
- audio_query: bfloat16 [2, 1024, 2048], P('groups', ('tok', 'head')), parts along dimension 0, may hold values from -640 to 640
- audio_key: bfloat16 [2, 1024, 2048], P('groups', ('tok', 'head')), parts along dimension 0, may hold values from -6 to 6
- audio_value: bfloat16 [2, 1024, 2048], P('groups', ('tok', 'head')), parts along dimension 0, may hold values from -6 to 6
- cross_audio_query: bfloat16 [2, 1024, 2048], P('groups', ('tok', 'head')), parts along dimension 0, may hold values from -640 to 640
- cross_video_key: bfloat16 [2, 4096, 2048], P('groups', ('tok', 'head')), parts along dimension 0, may hold values from -6 to 6
- cross_video_value: bfloat16 [2, 4096, 2048], P('groups', ('tok', 'head')), parts along dimension 0, may hold values from -6 to 6
- cross_video_query: bfloat16 [2, 4096, 2048], P('groups', ('tok', 'head')), parts along dimension 0, may hold values from -640 to 640
- cross_audio_key: bfloat16 [2, 1024, 2048], P('groups', ('tok', 'head')), parts along dimension 0, may hold values from -6 to 6
- cross_audio_value: bfloat16 [2, 1024, 2048], P('groups', ('tok', 'head')), parts along dimension 0, may hold values from -6 to 6
- audio_frames: int32 [2, 1024], P('groups', ('tok', 'head')), parts along dimension 0, may hold values from 0 to 15
- into_audio_slope: float32 [32], replicated, may hold values from 0.05 to 0.5
- into_video_slope: float32 [32], replicated, may hold values from 0.05 to 0.5
- timestep: int32 [2], P('groups'), parts along dimension 0, may hold values from 0 to 63
- video_gate: bfloat16 [64, 4096], replicated, may hold values from 2 to 12
- audio_gate: bfloat16 [64, 2048], replicated, may hold values from 2 to 12
- into_audio_gate: bfloat16 [64, 2048], replicated, may hold values from 2 to 12
- into_video_gate: bfloat16 [64, 2048], replicated, may hold values from 2 to 12
Outputs:
- video_self: bfloat16 [2, 4096, 4096], P('groups', ('tok', 'head')), parts along dimension 0
- audio_self: bfloat16 [2, 1024, 2048], P('groups', ('tok', 'head')), parts along dimension 0
- audio_cross: bfloat16 [2, 1024, 2048], P('groups', ('tok', 'head')), parts along dimension 0
- video_cross: bfloat16 [2, 4096, 2048], P('groups', ('tok', 'head')), parts along dimension 0
The draws below stay inside these ranges and needn't reach their ends.
There are 2 independent parts, one for each index of `groups`. The reference program is written for one: setup_inputs(seed, part) draws one part's arguments, and reference() takes and returns one part's arrays. A program takes and returns all parts, laid end to end along the dimension named above; an argument that names none is the same for every part. Nothing has to cross between parts.
All inputs are finite; a program needn't handle non-finite values.
Results may differ from the reference program's by a relative error of at most 0.0075.
Values may be sent and summed in bfloat16 or wider, within the bound.
No kernel may reach another device: no remote copies, remote signals or barrier semaphores. Data moves between devices by JAX's collectives and lax.ppermute only.
A program may use at most 128 MiB of HBM per device.

```python
import math
import jax
import jax.numpy as jnp
from jax import lax

SAMPLES = 1
LV = 4096
LA = 1024
FRAMES = 16
HV = 32
DHV = 128
HA = 32
DHA = 64
TSTEPS = 64
DV = 4096
DA = 2048


def paired_draw(key, query_count, key_count, heads_n, head_width, salt):
    folded = jax.random.fold_in(key, salt)
    streams = jax.random.split(folded, 2)
    columns = heads_n * head_width
    queries = jnp.clip(jax.random.normal(streams[0], (SAMPLES, query_count, columns), jnp.float32), -6.0, 6.0)
    keyed = 1.5 * jax.random.truncated_normal(streams[1], -4.0, 4.0, (SAMPLES, key_count, columns), jnp.float32)
    return (queries, keyed)


def draw_video_query(key, part):
    return paired_draw(key, LV, LV, HV, DHV, 11)[0].astype(jnp.bfloat16)


def draw_video_key(key, part):
    return paired_draw(key, LV, LV, HV, DHV, 11)[1].astype(jnp.bfloat16)


def draw_audio_query(key, part):
    return paired_draw(key, LA, LA, HA, DHA, 12)[0].astype(jnp.bfloat16)


def draw_audio_key(key, part):
    return paired_draw(key, LA, LA, HA, DHA, 12)[1].astype(jnp.bfloat16)


def draw_cross_audio_query(key, part):
    return paired_draw(key, LA, LV, HA, DHA, 13)[0].astype(jnp.bfloat16)


def draw_cross_video_key(key, part):
    return paired_draw(key, LA, LV, HA, DHA, 13)[1].astype(jnp.bfloat16)


def draw_cross_video_query(key, part):
    return paired_draw(key, LV, LA, HA, DHA, 14)[0].astype(jnp.bfloat16)


def draw_cross_audio_key(key, part):
    return paired_draw(key, LV, LA, HA, DHA, 14)[1].astype(jnp.bfloat16)


def place_ends(values, stream_key, low, high):
    longest = values.shape.index(max(values.shape))
    spots = []
    for shift in (0, 1):
        where = [jax.random.randint(jax.random.fold_in(stream_key, axis), (), 0, length) for axis, length in enumerate(values.shape)]
        where[longest] = (where[longest] + shift) % values.shape[longest]
        spots.append(tuple(where))
    return values.at[spots[0]].set(low).at[spots[1]].set(high)


def shard_levels(own_key, extent, pieces, least, largest):
    gain, own = 1.0, jax.random.fold_in(own_key, 6)
    for axis_at, blocks in pieces:
        draws = jnp.exp(jax.random.uniform(jax.random.fold_in(own, axis_at), (blocks,), jnp.float32, least / len(pieces), largest / len(pieces)))
        gain = gain * jnp.repeat(draws, extent[axis_at] // blocks).reshape([-1 if axis == axis_at else 1 for axis in range(len(extent))])
    return gain


def centred(own_key, extent, scale, bound, cuts=(), held_as=jnp.bfloat16):
    factor_of = shard_levels(own_key, extent, cuts, -0.22, 0.18) if cuts else 1.0
    entries = jax.random.normal(own_key, extent, jnp.float32) * scale * factor_of
    return jnp.minimum(jnp.maximum(entries, -bound), bound).astype(held_as)


def setup_inputs(seed: int = 0, part: int = 0) -> dict:
    key_list = jax.random.split(jax.random.key(seed), 21)
    own_keys = jax.random.split(jax.random.fold_in(key_list[20], part), 21)
    video_query = draw_video_query(jax.random.fold_in(jax.random.fold_in(key_list[20], part), 71), part)
    video_key = draw_video_key(jax.random.fold_in(jax.random.fold_in(key_list[20], part), 71), part)
    video_value = centred(own_keys[2], (SAMPLES, LV, DV), 1.0, 6.0, ((1, 16),))
    audio_query = draw_audio_query(jax.random.fold_in(jax.random.fold_in(key_list[20], part), 71), part)
    audio_key = draw_audio_key(jax.random.fold_in(jax.random.fold_in(key_list[20], part), 71), part)
    audio_value = centred(own_keys[5], (SAMPLES, LA, DA), 1.0, 6.0, ((1, 16),))
    cross_audio_query = draw_cross_audio_query(jax.random.fold_in(jax.random.fold_in(key_list[20], part), 71), part)
    cross_video_key = draw_cross_video_key(jax.random.fold_in(jax.random.fold_in(key_list[20], part), 71), part)
    cross_video_value = centred(own_keys[8], (SAMPLES, LV, DA), 1.0, 6.0, ((1, 16),))
    cross_video_query = draw_cross_video_query(jax.random.fold_in(jax.random.fold_in(key_list[20], part), 71), part)
    cross_audio_key = draw_cross_audio_key(jax.random.fold_in(jax.random.fold_in(key_list[20], part), 71), part)
    cross_audio_value = centred(own_keys[11], (SAMPLES, LA, DA), 1.0, 6.0, ((1, 16),))
    audio_frames = place_ends(jax.random.randint(own_keys[12], (SAMPLES, LA), 0, FRAMES), jax.random.fold_in(own_keys[12], 1), 0, FRAMES - 1).astype(jnp.int32)
    into_audio_slope = jnp.clip(jnp.exp(jax.random.uniform(key_list[13], (HA,), jnp.float32, math.log(0.05), math.log(0.5))), 0.05, 0.5)
    into_video_slope = jnp.clip(jnp.exp(jax.random.uniform(key_list[14], (HA,), jnp.float32, math.log(0.05), math.log(0.5))), 0.05, 0.5)
    timestep = jax.random.randint(own_keys[15], (SAMPLES,), 0, TSTEPS).astype(jnp.int32)
    video_gate = jnp.clip(jnp.exp(jax.random.uniform(key_list[16], (TSTEPS, DV), jnp.float32, math.log(2.0), math.log(12.0))), 2.0, 12.0).astype(jnp.bfloat16)
    audio_gate = jnp.clip(jnp.exp(jax.random.uniform(key_list[17], (TSTEPS, DA), jnp.float32, math.log(2.0), math.log(12.0))), 2.0, 12.0).astype(jnp.bfloat16)
    into_audio_gate = jnp.clip(jnp.exp(jax.random.uniform(key_list[18], (TSTEPS, DA), jnp.float32, math.log(2.0), math.log(12.0))), 2.0, 12.0).astype(jnp.bfloat16)
    into_video_gate = jnp.clip(jnp.exp(jax.random.uniform(key_list[19], (TSTEPS, DA), jnp.float32, math.log(2.0), math.log(12.0))), 2.0, 12.0).astype(jnp.bfloat16)
    return dict(video_query=video_query, video_key=video_key, video_value=video_value, audio_query=audio_query, audio_key=audio_key, audio_value=audio_value, cross_audio_query=cross_audio_query, cross_video_key=cross_video_key, cross_video_value=cross_video_value, cross_video_query=cross_video_query, cross_audio_key=cross_audio_key, cross_audio_value=cross_audio_value, audio_frames=audio_frames, into_audio_slope=into_audio_slope, into_video_slope=into_video_slope, timestep=timestep, video_gate=video_gate, audio_gate=audio_gate, into_audio_gate=into_audio_gate, into_video_gate=into_video_gate)


def attend_ref(queries, keyed, valued, heads_n, slopes, query_places, key_places):
    samples, counted, columns = queries.shape
    head_width = columns // heads_n
    score_scale = 1.0 / math.sqrt(head_width)

    def by_heads(tensor):
        return tensor.reshape(samples, tensor.shape[1], heads_n, head_width).transpose(2, 0, 1, 3)

    def one_head(packed):
        head_query_slice, head_key_slice, head_value_slice, slope_value = packed
        logit_scores = jnp.einsum('liv,lzv->liz', head_query_slice.astype(jnp.float32), head_key_slice.astype(jnp.float32)) * score_scale
        logit_scores = logit_scores - slope_value * jnp.abs(query_places[:, :, None] - key_places[:, None, :])
        maxima = lax.optimization_barrier(jnp.max(logit_scores, axis=2))
        exps = jnp.exp(logit_scores - maxima[:, :, None])
        totals = lax.optimization_barrier(jnp.sum(exps, axis=2))
        softmax_weights = exps.astype(jnp.bfloat16).astype(jnp.float32)
        weighted_sum = jnp.einsum('xpr,xre->xpe', softmax_weights, head_value_slice.astype(jnp.float32))
        return weighted_sum / totals[:, :, None]
    result = lax.map(one_head, (by_heads(queries), by_heads(keyed), by_heads(valued), slopes))
    return result.transpose(1, 2, 0, 3).reshape(samples, counted, columns)

def reference(video_query, video_key, video_value, audio_query, audio_key, audio_value, cross_audio_query, cross_video_key, cross_video_value, cross_video_query, cross_audio_key, cross_audio_value, audio_frames, into_audio_slope, into_video_slope, timestep, video_gate, audio_gate, into_audio_gate, into_video_gate):
    frame_of = (jnp.arange(LV, dtype=jnp.int32) // (LV // FRAMES)).astype(jnp.float32)
    video_time = jnp.broadcast_to(frame_of[None, :], (SAMPLES, LV))
    audio_time = audio_frames.astype(jnp.float32)
    still_video = jnp.zeros((SAMPLES, LV), jnp.float32)
    still_audio = jnp.zeros((SAMPLES, LA), jnp.float32)

    def gated(attended, table):
        factor = table[timestep].astype(jnp.float32)
        return (attended * factor[:, None, :]).astype(jnp.bfloat16)
    video_self = gated(attend_ref(video_query, video_key, video_value, HV, jnp.zeros((HV,), jnp.float32), still_video, still_video), video_gate)
    audio_self = gated(attend_ref(audio_query, audio_key, audio_value, HA, jnp.zeros((HA,), jnp.float32), still_audio, still_audio), audio_gate)
    audio_cross = gated(attend_ref(cross_audio_query, cross_video_key, cross_video_value, HA, into_audio_slope, audio_time, video_time), into_audio_gate)
    video_cross = gated(attend_ref(cross_video_query, cross_audio_key, cross_audio_value, HA, into_video_slope, video_time, audio_time), into_video_gate)
    return (video_self, audio_self, audio_cross, video_cross)
```

```python
import math

import jax
import jax.numpy as jnp
from jax import lax
from jax.experimental import pallas as pl
from jax.experimental.pallas import tpu as pltpu
from jax.sharding import PartitionSpec as P


LV = 4096
FRAMES = 16
DHV = 128
DHA = 64
LANES = 128
LOG2E = 1.4426950408889634
VIDEO_PARTS = 2


BF16 = jnp.bfloat16
F32 = jnp.float32


def swap(value, axis, mask):
    count = lax.axis_size(axis)
    return lax.ppermute(value, axis, [(j, j ^ mask) for j in range(count)])


def cost(flops, exps, moved):
    return pl.CostEstimate(flops=int(flops), transcendentals=int(exps), bytes_accessed=int(moved))


def nt(a, b):
    return lax.dot_general(a, b, (((1,), (1,)), ((), ())), preferred_element_type=F32)


def pack(arrays, tok_count, parts):
    rows, columns = arrays[0].shape
    wide = columns // tok_count
    part = wide // parts
    n = len(arrays)
    if part % LANES:
        me = lax.axis_index("tok")
        return [
            jnp.stack(
                [lax.dynamic_slice_in_dim(a, (me ^ m) * wide + p * part, part, 1) for a in arrays]
            )
            for p in range(parts)
            for m in range(tok_count)
        ]
    high = min(32, rows)

    def body(*refs):
        ins, outs = refs[:n], refs[n:]
        me = lax.axis_index("tok")
        for p in range(parts):
            for m in range(tok_count):
                start = pl.multiple_of((me ^ m) * wide + p * part, part)
                for a in range(n):
                    outs[p * tok_count + m][a] = ins[a][:, pl.ds(start, part)]

    count = tok_count * parts
    return pl.pallas_call(
        body,
        grid=(rows // high,),
        out_shape=[jax.ShapeDtypeStruct((n, rows, part), BF16)] * count,
        in_specs=[pl.BlockSpec((high, columns), lambda i: (i, 0))] * n,
        out_specs=[pl.BlockSpec((n, high, part), lambda i: (0, i, 0))] * count,
        cost_estimate=cost(0, 0, 4 * n * rows * columns),
        name="pack",
    )(*arrays)


def assemble(blocks):
    count = len(blocks)
    _, rows, wide = blocks[0].shape
    high = min(64, rows)

    def body(*refs):
        for m in range(count):
            for a in range(2):
                refs[count][a, m] = refs[m][a]

    joined = pl.pallas_call(
        body,
        grid=(rows // high,),
        out_shape=jax.ShapeDtypeStruct((2, count, rows, wide), BF16),
        in_specs=[pl.BlockSpec((2, high, wide), lambda i: (0, i, 0))] * count,
        out_specs=pl.BlockSpec((2, count, high, wide), lambda i: (0, 0, i, 0)),
        cost_estimate=cost(0, 0, 8 * count * rows * wide),
        name="assemble",
    )(*blocks)
    return joined.reshape(2, count * rows, wide)


def unpack(parts, tok_count):
    count = len(parts)
    rows, part = parts[0][0].shape
    wide = part * count
    if part % LANES:
        me = lax.axis_index("tok")
        out = jnp.zeros((rows, wide * tok_count), BF16)
        for p in range(count):
            for m in range(tok_count):
                at = (me ^ m) * wide + p * part
                out = lax.dynamic_update_slice_in_dim(out, parts[p][m], at, 1)
        return out
    high = min(32, rows)

    def body(*refs):
        me = lax.axis_index("tok")
        out = refs[-1]
        for p in range(count):
            for m in range(tok_count):
                start = pl.multiple_of((me ^ m) * wide + p * part, part)
                out[:, pl.ds(start, part)] = refs[p * tok_count + m][...]

    return pl.pallas_call(
        body,
        grid=(rows // high,),
        out_shape=jax.ShapeDtypeStruct((rows, wide * tok_count), BF16),
        in_specs=[pl.BlockSpec((high, part), lambda i: (i, 0))] * (count * tok_count),
        out_specs=pl.BlockSpec((high, wide * tok_count), lambda i: (i, 0)),
        cost_estimate=cost(0, 0, 4 * rows * wide * tok_count),
        name="unpack",
    )(*[block for blocks in parts for block in blocks])


def stack_rows(first, second):
    rows, wide = first.shape

    def body(a_ref, b_ref, out_ref):
        out_ref[:rows] = a_ref[...]
        out_ref[rows:] = b_ref[...]

    return pl.pallas_call(
        body,
        out_shape=jax.ShapeDtypeStruct((2 * rows, wide), BF16),
        cost_estimate=cost(0, 0, 8 * rows * wide),
        name="stack_rows",
    )(first, second)


def lane_of(shape):
    return lax.broadcasted_iota(jnp.int32, shape, len(shape) - 1)


def one_head(queries, parts, scale):
    factor = scale * LOG2E
    top = total = summed = None
    for keys, values in parts:
        scores = nt(queries, keys)
        peak = jnp.max(scores, axis=1, keepdims=True)
        new_top = peak if top is None else jnp.maximum(top, peak)
        exps = jnp.exp2((scores - new_top) * factor)
        sums = jnp.sum(exps, axis=1, keepdims=True)
        part = jnp.dot(exps.astype(BF16), values, preferred_element_type=F32)
        if top is None:
            total, summed = sums, part
        else:
            fade = jnp.exp2((top - new_top) * factor)
            total = total * fade + sums
            summed = summed * fade + part
        top = new_top
    return total, summed


def pick(lanes, width, keys, index):
    if lanes == width:
        return keys
    here = (lane_of(keys.shape) // width) == index
    return jnp.where(here, keys, jnp.zeros_like(keys))


def self_attention(blocks, own, other, gate, width):
    tok_count = len(blocks)
    _, rows, columns = blocks[0].shape
    counted = rows * tok_count
    keyed = own.shape[1]
    lanes = min(LANES, columns)
    heads = lanes // width
    block = min(512, counted)
    chunk = min(1024, keyed)
    scale = 1.0 / math.sqrt(width)

    def body(*refs):
        q_refs, (own_ref, other_ref, gate_ref) = refs[:tok_count], refs[tok_count : tok_count + 3]
        outs, (q_held, held) = refs[tok_count + 3 : -2], refs[-2:]
        gates = gate_ref[...]
        for m in range(tok_count):
            q_held[m * rows : (m + 1) * rows, :] = q_refs[m][0]

        def step(b, carry):
            at = pl.multiple_of(b * block, block)
            q = q_held[pl.ds(at, block), :]
            result = None
            for head in range(heads):
                parts = []
                for ref in (own_ref, other_ref):
                    for c in range(keyed // chunk):
                        here = pl.ds(c * chunk, chunk)
                        keys = pick(lanes, width, ref[0, here, :], head)
                        parts.append((keys, ref[1, here, :]))
                total, summed = one_head(q, parts, scale)
                done = summed / total
                if result is None:
                    result = done
                else:
                    result = jnp.where(lane_of(done.shape) // width == head, done, result)
            held[pl.ds(at, block), :] = (result * gates).astype(BF16)
            return carry

        lax.fori_loop(0, counted // block, step, 0)
        for m in range(tok_count):
            outs[m][...] = held[m * rows : (m + 1) * rows, :]

    steps = columns // lanes
    scores = counted * keyed * 2 * (columns // width)
    return pl.pallas_call(
        body,
        grid=(steps,),
        out_shape=[jax.ShapeDtypeStruct((rows, columns), BF16)] * tok_count,
        in_specs=[pl.BlockSpec((1, rows, lanes), lambda i: (2, 0, i))] * tok_count
        + [
            pl.BlockSpec((2, keyed, lanes), lambda i: (0, 0, i)),
            pl.BlockSpec((2, keyed, lanes), lambda i: (0, 0, i)),
            pl.BlockSpec((1, lanes), lambda i: (0, i)),
        ],
        out_specs=[pl.BlockSpec((rows, lanes), lambda i: (0, i))] * tok_count,
        scratch_shapes=[pltpu.VMEM((counted, lanes), BF16)] * 2,
        cost_estimate=cost(scores * 4 * LANES, scores, 2 * columns * (2 * counted + 4 * keyed)),
        name="self_attention",
    )(*blocks, own, other, gate)


def video_cross_local(queries, pieces, slopes, gate, place, span):
    counted, columns = queries.shape
    keyed = pieces[0].shape[0]
    n = len(pieces)
    steps = columns // LANES
    heads = LANES // DHA
    factor = LOG2E / math.sqrt(DHA)

    def body(slope_ref, place_ref, q_ref, *refs):
        gate_ref, out_ref = refs[3 * n :]
        i = pl.program_id(0)
        q = q_ref[...]
        at = place_ref[0]
        if span % counted == 0:
            mine = (at // span).astype(F32)
        else:
            col = lax.broadcasted_iota(jnp.int32, (1, counted), 1)
            mine = ((at + col) // span).astype(F32)
        gaps, turned = [], []
        for p in range(n):
            frame = refs[3 * p + 2][...].astype(F32)
            if counted > LANES:
                frame = jnp.concatenate([frame] * (counted // LANES), axis=1)
            gaps.append(jnp.abs(frame[:, :counted] - mine))
            turned.append(jnp.transpose(refs[3 * p + 1][...]))
        results = []
        for head in range(heads):
            slope = slope_ref[i * heads + head] * LOG2E
            scores = [
                nt(pick(LANES, DHA, refs[3 * p][...], head), q) * factor - gaps[p] * slope
                for p in range(n)
            ]
            top = jnp.max(scores[0], axis=0, keepdims=True)
            for one in scores[1:]:
                top = jnp.maximum(top, jnp.max(one, axis=0, keepdims=True))
            total = summed = None
            for p in range(n):
                exps = jnp.exp2(scores[p] - top)
                sums = jnp.sum(exps, axis=0, keepdims=True)
                part = jnp.dot(
                    turned[p][head * DHA : (head + 1) * DHA],
                    exps.astype(BF16),
                    preferred_element_type=F32,
                )
                total = sums if total is None else total + sums
                summed = part if summed is None else summed + part
            results.append(summed / total)
        result = jnp.transpose(jnp.concatenate(results, axis=0))
        out_ref[...] = (result * gate_ref[...]).astype(BF16)

    piece = [
        pl.BlockSpec((keyed, LANES), lambda i: (0, steps + i)),
        pl.BlockSpec((keyed, LANES), lambda i: (0, 2 * steps + i)),
        pl.BlockSpec((keyed, LANES), lambda i: (0, 3 * steps)),
    ]
    scores = counted * keyed * n * steps * heads
    return pl.pallas_call(
        body,
        grid=(steps,),
        out_shape=jax.ShapeDtypeStruct((counted, columns), BF16),
        in_specs=[
            pl.BlockSpec(memory_space=pltpu.SMEM),
            pl.BlockSpec(memory_space=pltpu.SMEM),
            pl.BlockSpec((counted, LANES), lambda i: (0, i)),
        ]
        + piece * n
        + [pl.BlockSpec((1, LANES), lambda i: (0, i))],
        out_specs=pl.BlockSpec((counted, LANES), lambda i: (0, i)),
        cost_estimate=cost(scores * 4 * LANES, scores, 4 * columns * (counted + n * keyed)),
        name="video_cross",
    )(slopes, place, queries, *[a for piece in pieces for a in (piece, piece, piece)], gate)


def audio_cross_local(pieces, keys, values, slopes, place, span):
    counted = pieces[0].shape[0]
    n = len(pieces)
    keyed, columns = keys.shape
    steps = columns // LANES
    heads = LANES // DHA
    count = steps * heads
    factor = LOG2E / math.sqrt(DHA)

    def body(slope_ref, place_ref, k_ref, v_ref, *refs):
        q_refs, f_refs, o_refs = refs[:n], refs[n : 2 * n], refs[2 * n : 3 * n]
        stats, times = refs[3 * n :]
        i = pl.program_id(0)
        at = place_ref[0]

        @pl.when(i == 0)
        def _():
            stats[...] = jnp.zeros_like(stats)
            for p in range(n):
                times[p] = jnp.transpose(f_refs[p][...].astype(F32))[0:8, :]

        @pl.when(i < steps)
        def _():
            keys_here = k_ref[...]
            turned = jnp.transpose(v_ref[...])
            for p in range(n):
                q = q_refs[p][...]
                mine = times[p, 0:1, :]
                if span % keyed == 0:
                    gap = jnp.abs(mine - (at // span).astype(F32))
                else:
                    row = lax.broadcasted_iota(jnp.int32, (keyed, 1), 0)
                    gap = jnp.abs(mine - ((at + row) // span).astype(F32))
                results = []
                for head in range(heads):
                    index = i * heads + head
                    slope = slope_ref[index] * LOG2E
                    scores = nt(pick(LANES, DHA, keys_here, head), q)
                    if span % keyed == 0:
                        top = jnp.max(scores, axis=0, keepdims=True)
                        exps = jnp.exp2((scores - top) * factor)
                        top = top * factor - gap * slope
                    else:
                        scores = scores * factor - gap * slope
                        top = jnp.max(scores, axis=0, keepdims=True)
                        exps = jnp.exp2(scores - top)
                    total = jnp.sum(exps, axis=0, keepdims=True)
                    part = jnp.dot(
                        turned[head * DHA : (head + 1) * DHA],
                        exps.astype(BF16),
                        preferred_element_type=F32,
                    )
                    results.append(part / total)
                    stats[p, pl.ds(index, 1), :] = top + jnp.log2(total)
                result = jnp.concatenate(results, axis=0)
                o_refs[p][...] = jnp.transpose(result).astype(BF16)

        @pl.when(i == steps)
        def _():
            for p in range(n):
                o_refs[p][...] = spread_stats(jnp.transpose(stats[p]), count)

    def at_step(i):
        return jnp.minimum(i, steps - 1)

    scores = counted * keyed * n * count
    return pl.pallas_call(
        body,
        grid=(steps + 1,),
        out_shape=[jax.ShapeDtypeStruct((counted, columns + LANES), BF16)] * n,
        in_specs=[
            pl.BlockSpec(memory_space=pltpu.SMEM),
            pl.BlockSpec(memory_space=pltpu.SMEM),
        ]
        + [pl.BlockSpec((keyed, LANES), lambda i: (0, at_step(i)))] * 2
        + [pl.BlockSpec((counted, LANES), lambda i: (0, at_step(i)))] * n
        + [pl.BlockSpec((counted, LANES), lambda i: (0, 3 * steps))] * n,
        out_specs=[pl.BlockSpec((counted, LANES), lambda i: (0, i))] * n,
        scratch_shapes=[
            pltpu.VMEM((n, LANES, counted), F32),
            pltpu.VMEM((n, 8, counted), F32),
        ],
        cost_estimate=cost(scores * 4 * LANES, scores, 4 * columns * (n * counted + keyed)),
        name="audio_cross",
    )(slopes, place, keys, values, *pieces, *pieces)


def spread_stats(stats, count):
    lane = lane_of(stats.shape)
    first = stats.astype(BF16).astype(F32)
    rest = stats - first
    second = rest.astype(BF16).astype(F32)
    third = rest - second
    second = pltpu.roll(second, count, 1)
    third = pltpu.roll(third, 2 * count, 1)
    packed = jnp.where(lane < count, first, jnp.where(lane < 2 * count, second, third))
    return jnp.where(lane < 3 * count, packed, 0.0).astype(BF16)


def read_stats(packed, count):
    terms = packed.astype(F32)
    second = pltpu.roll(terms, LANES - count, 1)
    third = pltpu.roll(terms, LANES - 2 * count, 1)
    return terms + second + third


def merge(mine, theirs, form, gate=None):
    rows, wide = mine.shape
    columns = wide - LANES
    count = columns // DHA
    heads = LANES // DHA
    half = rows // 2

    def body(a_ref, b_ref, *refs):
        a_stat = read_stats(a_ref[:, columns:], count)
        b_stat = read_stats(b_ref[:, columns:], count)
        top = jnp.maximum(a_stat, b_stat)
        a_part = jnp.exp2(a_stat - top)
        b_part = jnp.exp2(b_stat - top)
        total = a_part + b_part
        a_share = a_part / total
        b_share = b_part / total
        lane = lane_of((rows, LANES)) // DHA

        def put(here, value):
            if form == "halves":
                refs[0][:, here] = value[:half]
                refs[1][:, here] = value[half:]
            else:
                refs[-1][:, here] = value

        for j in range(columns // LANES):
            here = slice(j * LANES, (j + 1) * LANES)
            a_weight = a_share[:, j * heads : j * heads + 1]
            b_weight = b_share[:, j * heads : j * heads + 1]
            for h in range(1, heads):
                at = j * heads + h
                a_weight = jnp.where(lane == h, a_share[:, at : at + 1], a_weight)
                b_weight = jnp.where(lane == h, b_share[:, at : at + 1], b_weight)
            joined = a_ref[:, here].astype(F32) * a_weight + b_ref[:, here].astype(F32) * b_weight
            if form == "last":
                joined = joined * refs[0][:, here]
            put(here, joined.astype(BF16))
        if form != "last":
            put(slice(columns, wide), spread_stats(top + jnp.log2(total), count))

    if form == "halves":
        shapes = [jax.ShapeDtypeStruct((half, wide), BF16)] * 2
    elif form == "last":
        shapes = jax.ShapeDtypeStruct((rows, columns), BF16)
    else:
        shapes = jax.ShapeDtypeStruct((rows, wide), BF16)
    extra = () if gate is None else (gate,)
    return pl.pallas_call(
        body,
        out_shape=shapes,
        cost_estimate=cost(0, rows * wide, 6 * rows * wide),
        name="merge",
    )(mine, theirs, *extra)


def on_device(
    video_query,
    video_key,
    video_value,
    audio_query,
    audio_key,
    audio_value,
    cross_audio_query,
    cross_video_key,
    cross_video_value,
    cross_video_query,
    cross_audio_key,
    cross_audio_value,
    audio_frames,
    into_audio_slope,
    into_video_slope,
    timestep,
    video_gate,
    audio_gate,
    into_audio_gate,
    into_video_gate,
):
    tok_count = lax.axis_size("tok")
    head_count = lax.axis_size("head")
    tok = lax.axis_index("tok")
    samples, video_rows, video_columns = video_query.shape
    audio_rows, _ = audio_query.shape[1:]
    patches = LV // FRAMES
    place = ((tok * head_count + lax.axis_index("head")) * video_rows).reshape(1)
    masks = [1 << b for b in reversed(range(tok_count.bit_length() - 1))]

    def gate_row(table, sample):
        return lax.dynamic_slice_in_dim(table, timestep[sample], 1, 0).astype(F32)

    def gate_part(row, part, parts):
        wide = row.shape[1] // tok_count
        piece = wide // parts
        return lax.dynamic_slice_in_dim(row, tok * wide + part * piece, piece, 1)

    def exchange(blocks):
        return [blocks[0]] + [swap(blocks[m], "tok", m) for m in range(1, tok_count)]

    def self_part(blocks, gate, width):
        blocks = exchange(blocks)
        own = assemble(blocks)
        other = swap(own, "head", 1)
        outs = self_attention(blocks, own, other, gate, width)
        return exchange(outs)

    results = []
    for s in range(samples):
        frames = jnp.broadcast_to(
            audio_frames[s][:, None].astype(F32), (audio_rows, LANES)
        ).astype(BF16)
        own = jnp.concatenate(
            (cross_audio_query[s], cross_audio_key[s], cross_audio_value[s], frames), axis=1
        )
        for step, mask in enumerate(masks):
            received = swap(own, "tok", mask)
            if step < len(masks) - 1:
                own = stack_rows(own, received)
        pieces = [own, received, swap(own, "head", 1), swap(received, "head", 1)]
        partial = audio_cross_local(
            pieces, cross_video_key[s], cross_video_value[s], into_audio_slope, place, patches
        )
        got = [swap(partial[2], "head", 1), swap(partial[3], "head", 1)]
        mine = merge(partial[0], got[0], "whole")
        send = merge(partial[1], got[1], "whole")
        for step, mask in enumerate(reversed(masks)):
            received = swap(send, "tok", mask)
            if step < len(masks) - 1:
                mine, send = merge(mine, received, "halves")
            else:
                audio_cross = merge(mine, received, "last", gate_row(into_audio_gate, s))
        blocks = pack((audio_key[s], audio_value[s], audio_query[s]), tok_count, 1)
        gate = gate_row(audio_gate, s)
        outs = self_part(blocks, gate_part(gate, 0, 1), DHA)
        audio_self = unpack([outs], tok_count)
        wide = video_columns // tok_count
        parts = VIDEO_PARTS if wide % (VIDEO_PARTS * LANES) == 0 else 1
        blocks = pack((video_key[s], video_value[s], video_query[s]), tok_count, parts)
        gate = gate_row(video_gate, s)
        outs = []
        for p in range(parts):
            mine = blocks[p * tok_count : (p + 1) * tok_count]
            outs.append(self_part(mine, gate_part(gate, p, parts), DHV))
        video_self = unpack(outs, tok_count)
        video_cross = video_cross_local(
            cross_video_query[s],
            pieces,
            into_video_slope,
            gate_row(into_video_gate, s),
            place,
            patches,
        )
        results.append((video_self, audio_self, audio_cross, video_cross))
    return tuple(jnp.stack(parts) for parts in zip(*results))


def solution(mesh):
    rows = P("groups", ("tok", "head"), None)
    placed = (rows,) * 12 + (
        P("groups", ("tok", "head")),
        P(),
        P(),
        P("groups"),
        P(),
        P(),
        P(),
        P(),
    )

    return jax.shard_map(
        on_device, mesh=mesh, in_specs=placed, out_specs=(rows,) * 4, check_vma=False
    )
```

```python
import math

import jax
import jax.numpy as jnp
from jax import lax
from jax.experimental import pallas as pl
from jax.experimental.pallas import tpu as pltpu
from jax.sharding import PartitionSpec as P


LV = 4096
FRAMES = 16
DHV = 128
DHA = 64
LANES = 128
LOG2E = 1.4426950408889634
VIDEO_PARTS = 2


BF16 = jnp.bfloat16
F32 = jnp.float32


def swap(value, axis, mask):
    count = lax.axis_size(axis)
    return lax.ppermute(value, axis, [(j, j ^ mask) for j in range(count)])


def cost(flops, exps, moved):
    return pl.CostEstimate(flops=int(flops), transcendentals=int(exps), bytes_accessed=int(moved))


def nt(a, b):
    return lax.dot_general(a, b, (((1,), (1,)), ((), ())), preferred_element_type=F32)


def pack(entries, tok_count):
    rows = [a.shape[0] for a, _, _ in entries]
    wide = entries[0][0].shape[1] // tok_count // entries[0][2]
    n = len(entries)
    if wide % LANES:
        cut = [
            a.reshape(a.shape[0], tok_count, parts, wide)[:, :, part].transpose(1, 0, 2)
            for a, part, parts in entries
        ]
        return jnp.concatenate(cut, axis=1)

    def body(*refs):
        at = 0
        for a in range(n):
            refs[n][0, at : at + rows[a], :] = refs[a][...]
            at += rows[a]

    total = sum(rows)
    return pl.pallas_call(
        body,
        grid=(tok_count,),
        out_shape=jax.ShapeDtypeStruct((tok_count, total, wide), BF16),
        in_specs=[
            pl.BlockSpec((a.shape[0], wide), lambda m, p=part, q=parts: (0, m * q + p))
            for a, part, parts in entries
        ],
        out_specs=pl.BlockSpec((1, total, wide), lambda m: (m, 0, 0)),
        cost_estimate=cost(0, 0, 4 * total * tok_count * wide),
        name="pack",
    )(*[a for a, _, _ in entries])


def unpack(sources, rows):
    tok_count = sources[0][0][0].shape[0]
    wides = [entry[0][0].shape[2] for entry in sources]
    parts = [len(entry) for entry in sources]
    if any(w % LANES for w in wides):
        outs = []
        for entry, r, w in zip(sources, rows, wides):
            cut = [array[:, at : at + r].transpose(1, 0, 2) for array, at in entry]
            outs.append(jnp.stack(cut, axis=2).reshape(r, tok_count * len(entry) * w))
        return outs

    def body(*refs):
        at = 0
        for e, (w, count) in enumerate(zip(wides, parts)):
            out = refs[sum(parts) + e]
            for p in range(count):
                out[:, p * w : (p + 1) * w] = refs[at][0]
                at += 1

    flat = [(array, at, r) for entry, r in zip(sources, rows) for array, at in entry]
    for _, at, r in flat:
        assert at % r == 0
    return pl.pallas_call(
        body,
        grid=(tok_count,),
        out_shape=[
            jax.ShapeDtypeStruct((r, tok_count * w * count), BF16)
            for r, w, count in zip(rows, wides, parts)
        ],
        in_specs=[
            pl.BlockSpec((1, r, array.shape[2]), lambda m, k=at // r: (m, k, 0))
            for array, at, r in flat
        ],
        out_specs=[
            pl.BlockSpec((r, w * count), lambda m: (0, m))
            for r, w, count in zip(rows, wides, parts)
        ],
        cost_estimate=cost(0, 0, 4 * sum(r * w for r, w in zip(rows, wides)) * tok_count),
        name="unpack",
    )(*[array for array, _, _ in flat])


def stack_rows(first, second):
    rows, wide = first.shape

    def body(a_ref, b_ref, out_ref):
        out_ref[:rows] = a_ref[...]
        out_ref[rows:] = b_ref[...]

    return pl.pallas_call(
        body,
        out_shape=jax.ShapeDtypeStruct((2 * rows, wide), BF16),
        cost_estimate=cost(0, 0, 8 * rows * wide),
        name="stack_rows",
    )(first, second)


def lane_of(shape):
    return lax.broadcasted_iota(jnp.int32, shape, len(shape) - 1)


def one_head(queries, parts, scale):
    factor = scale * LOG2E
    top = total = summed = None
    for keys, values in parts:
        scores = nt(queries, keys)
        peak = jnp.max(scores, axis=1, keepdims=True)
        new_top = peak if top is None else jnp.maximum(top, peak)
        exps = jnp.exp2((scores - new_top) * factor)
        sums = jnp.sum(exps, axis=1, keepdims=True)
        part = jnp.dot(exps.astype(BF16), values, preferred_element_type=F32)
        if top is None:
            total, summed = sums, part
        else:
            fade = jnp.exp2((top - new_top) * factor)
            total = total * fade + sums
            summed = summed * fade + part
        top = new_top
    return total, summed


def pick(lanes, width, keys, index):
    if lanes == width:
        return keys
    here = (lane_of(keys.shape) // width) == index
    return jnp.where(here, keys, jnp.zeros_like(keys))


def self_attention(own, other, segments):
    tok_count, total, columns = own.shape
    lanes = min(LANES, columns)

    def body(*refs):
        out_ref = refs[-1]
        row_at = 0
        for g, (rows, width, _) in enumerate(segments):
            key_a, value_a, q_ref, key_b, value_b, gate_ref = refs[6 * g : 6 * g + 6]
            gates = gate_ref[...]
            heads = lanes // width
            scale = 1.0 / math.sqrt(width)
            some = max(1, min(tok_count, 512 // rows))
            span = max(1, min(tok_count, 1024 // rows))
            here = slice(row_at, row_at + rows)
            row_at += rows

            def step(b, carry):
                at = b * some
                q = q_ref[pl.ds(at, some)].reshape(some * rows, lanes)
                result = None
                for head in range(heads):
                    parts = []
                    for keys, values in ((key_a, value_a), (key_b, value_b)):
                        for c in range(0, tok_count, span):
                            k = keys[c : c + span].reshape(span * rows, lanes)
                            v = values[c : c + span].reshape(span * rows, lanes)
                            parts.append((pick(lanes, width, k, head), v))
                    whole, summed = one_head(q, parts, scale)
                    done = summed / whole
                    if result is None:
                        result = done
                    else:
                        result = jnp.where(lane_of(done.shape) // width == head, done, result)
                result = (result * gates).astype(BF16)
                out_ref[pl.ds(at, some), here, :] = result.reshape(some, rows, lanes)
                return carry

            lax.fori_loop(0, tok_count // some, step, 0)

    in_specs, operands = [], []
    scores = base = 0
    for rows, width, gate in segments:
        assert base % rows == 0
        first = base // rows
        for array, which in ((own, 0), (own, 1), (own, 2), (other, 0), (other, 1)):
            in_specs.append(
                pl.BlockSpec((tok_count, rows, lanes), lambda i, k=first + which: (0, k, i))
            )
            operands.append(array)
        in_specs.append(pl.BlockSpec((1, lanes), lambda i: (0, i)))
        operands.append(gate)
        scores += (tok_count * rows) ** 2 * 2 * (columns // width)
        base += 3 * rows
    out_rows = sum(rows for rows, _, _ in segments)
    return pl.pallas_call(
        body,
        grid=(columns // lanes,),
        out_shape=jax.ShapeDtypeStruct((tok_count, out_rows, columns), BF16),
        in_specs=in_specs,
        out_specs=pl.BlockSpec((tok_count, out_rows, lanes), lambda i: (0, 0, i)),
        cost_estimate=cost(scores * 4 * LANES, scores, 10 * tok_count * total * columns),
        name="self_attention",
    )(*operands)


def video_cross_local(queries, pieces, marks, slopes, gate, place, span):
    counted, columns = queries.shape
    keyed = pieces[0].shape[0]
    n = len(pieces)
    steps = columns // LANES
    heads = LANES // DHA
    factor = LOG2E / math.sqrt(DHA)

    def body(slope_ref, place_ref, q_ref, *refs):
        gate_ref, out_ref = refs[3 * n :]
        i = pl.program_id(0)
        q = q_ref[...]
        at = place_ref[0]
        if span % counted == 0:
            mine = (at // span).astype(F32)
        else:
            col = lax.broadcasted_iota(jnp.int32, (1, counted), 1)
            mine = ((at + col) // span).astype(F32)
        gaps, turned = [], []
        for p in range(n):
            frame = refs[3 * p + 2][...].astype(F32)
            if counted > LANES:
                frame = jnp.concatenate([frame] * (counted // LANES), axis=1)
            gaps.append(jnp.abs(frame[:, :counted] - mine))
            turned.append(jnp.transpose(refs[3 * p + 1][...]))
        results = []
        for head in range(heads):
            slope = slope_ref[i * heads + head] * LOG2E
            scores = [
                nt(pick(LANES, DHA, refs[3 * p][...], head), q) * factor - gaps[p] * slope
                for p in range(n)
            ]
            top = jnp.max(scores[0], axis=0, keepdims=True)
            for one in scores[1:]:
                top = jnp.maximum(top, jnp.max(one, axis=0, keepdims=True))
            total = summed = None
            for p in range(n):
                exps = jnp.exp2(scores[p] - top)
                sums = jnp.sum(exps, axis=0, keepdims=True)
                part = jnp.dot(
                    turned[p][head * DHA : (head + 1) * DHA],
                    exps.astype(BF16),
                    preferred_element_type=F32,
                )
                total = sums if total is None else total + sums
                summed = part if summed is None else summed + part
            results.append(summed / total)
        result = jnp.transpose(jnp.concatenate(results, axis=0))
        out_ref[...] = (result * gate_ref[...]).astype(BF16)

    piece = [
        pl.BlockSpec((keyed, LANES), lambda i: (0, i)),
        pl.BlockSpec((keyed, LANES), lambda i: (0, steps + i)),
        pl.BlockSpec((keyed, LANES), lambda i: (0, steps)),
    ]
    scores = counted * keyed * n * steps * heads
    return pl.pallas_call(
        body,
        grid=(steps,),
        out_shape=jax.ShapeDtypeStruct((counted, columns), BF16),
        in_specs=[
            pl.BlockSpec(memory_space=pltpu.SMEM),
            pl.BlockSpec(memory_space=pltpu.SMEM),
            pl.BlockSpec((counted, LANES), lambda i: (0, i)),
        ]
        + piece * n
        + [pl.BlockSpec((1, LANES), lambda i: (0, i))],
        out_specs=pl.BlockSpec((counted, LANES), lambda i: (0, i)),
        cost_estimate=cost(scores * 4 * LANES, scores, 4 * columns * (counted + n * keyed)),
        name="video_cross",
    )(slopes, place, queries, *[a for k, f in zip(pieces, marks) for a in (k, k, f)], gate)


def audio_cross_local(pieces, keys, values, slopes, place, span):
    counted = pieces[0].shape[0]
    n = len(pieces)
    keyed, columns = keys.shape
    steps = columns // LANES
    heads = LANES // DHA
    count = steps * heads
    factor = LOG2E / math.sqrt(DHA)

    def body(slope_ref, place_ref, k_ref, v_ref, *refs):
        q_refs, f_refs, o_refs = refs[:n], refs[n : 2 * n], refs[2 * n : 3 * n]
        stats, times = refs[3 * n :]
        i = pl.program_id(0)
        at = place_ref[0]

        @pl.when(i == 0)
        def _():
            stats[...] = jnp.zeros_like(stats)
            for p in range(n):
                here = slice(p * counted, (p + 1) * counted)
                times[:, here] = jnp.transpose(f_refs[p][...].astype(F32))[0:8, :]

        @pl.when(i < steps)
        def _():
            keys_here = k_ref[...]
            turned = jnp.transpose(v_ref[...])
            q = jnp.concatenate([r[...] for r in q_refs], axis=0)
            mine = times[0:1, :]
            if span % keyed == 0:
                gap = jnp.abs(mine - (at // span).astype(F32))
            else:
                row = lax.broadcasted_iota(jnp.int32, (keyed, 1), 0)
                gap = jnp.abs(mine - ((at + row) // span).astype(F32))
            results = []
            for head in range(heads):
                index = i * heads + head
                slope = slope_ref[index] * LOG2E
                scores = nt(pick(LANES, DHA, keys_here, head), q)
                if span % keyed == 0:
                    top = jnp.max(scores, axis=0, keepdims=True)
                    exps = jnp.exp2((scores - top) * factor)
                    top = top * factor - gap * slope
                else:
                    scores = scores * factor - gap * slope
                    top = jnp.max(scores, axis=0, keepdims=True)
                    exps = jnp.exp2(scores - top)
                total = jnp.sum(exps, axis=0, keepdims=True)
                part = jnp.dot(
                    turned[head * DHA : (head + 1) * DHA],
                    exps.astype(BF16),
                    preferred_element_type=F32,
                )
                results.append(part * (1.0 / total))
                stats[pl.ds(index, 1), :] = top + jnp.log2(total)
            result = jnp.transpose(jnp.concatenate(results, axis=0).astype(BF16))
            for p in range(n):
                o_refs[p][...] = result[p * counted : (p + 1) * counted]

        @pl.when(i == steps)
        def _():
            for p in range(n):
                here = slice(p * counted, (p + 1) * counted)
                o_refs[p][...] = spread_stats(jnp.transpose(stats[:, here]), count)

    def at_step(i):
        return jnp.minimum(i, steps - 1)

    scores = counted * keyed * n * count
    return pl.pallas_call(
        body,
        grid=(steps + 1,),
        out_shape=[jax.ShapeDtypeStruct((counted, columns + LANES), BF16)] * n,
        in_specs=[
            pl.BlockSpec(memory_space=pltpu.SMEM),
            pl.BlockSpec(memory_space=pltpu.SMEM),
        ]
        + [pl.BlockSpec((keyed, LANES), lambda i: (0, at_step(i)))] * 2
        + [pl.BlockSpec((counted, LANES), lambda i: (0, at_step(i)))] * n
        + [pl.BlockSpec((counted, LANES), lambda i: (0, steps))] * n,
        out_specs=[pl.BlockSpec((counted, LANES), lambda i: (0, i))] * n,
        scratch_shapes=[
            pltpu.VMEM((LANES, n * counted), F32),
            pltpu.VMEM((8, n * counted), F32),
        ],
        cost_estimate=cost(scores * 4 * LANES, scores, 4 * columns * (n * counted + keyed)),
        name="audio_cross",
    )(slopes, place, keys, values, *pieces, *pieces)


def spread_stats(stats, count):
    lane = lane_of(stats.shape)
    first = stats.astype(BF16).astype(F32)
    rest = stats - first
    second = rest.astype(BF16).astype(F32)
    third = rest - second
    second = pltpu.roll(second, count, 1)
    third = pltpu.roll(third, 2 * count, 1)
    packed = jnp.where(lane < count, first, jnp.where(lane < 2 * count, second, third))
    return jnp.where(lane < 3 * count, packed, 0.0).astype(BF16)


def read_stats(packed, count):
    terms = packed.astype(F32)
    second = pltpu.roll(terms, LANES - count, 1)
    third = pltpu.roll(terms, LANES - 2 * count, 1)
    return terms + second + third


def merge(mine, theirs, form, gate=None):
    rows, wide = mine.shape
    columns = wide - LANES
    count = columns // DHA
    heads = LANES // DHA
    half = rows // 2

    def body(a_ref, b_ref, *refs):
        a_stat = read_stats(a_ref[:, columns:], count)
        b_stat = read_stats(b_ref[:, columns:], count)
        top = jnp.maximum(a_stat, b_stat)
        a_part = jnp.exp2(a_stat - top)
        total = a_part + jnp.exp2(b_stat - top)
        share = a_part / total
        high = share.astype(BF16)
        low = (share - high.astype(F32)).astype(BF16)

        def put(here, value):
            if form == "halves":
                refs[0][:, here] = value[:half]
                refs[1][:, here] = value[half:]
            else:
                refs[-1][:, here] = value

        for j in range(columns // LANES):
            here = slice(j * LANES, (j + 1) * LANES)
            row = lax.broadcasted_iota(jnp.int32, (LANES, LANES), 0)
            spot = (row == j * heads + lane_of((LANES, LANES)) // DHA).astype(F32).astype(BF16)
            weight = jnp.dot(high, spot, preferred_element_type=F32)
            weight = weight + jnp.dot(low, spot, preferred_element_type=F32)
            theirs_here = b_ref[:, here].astype(F32)
            joined = theirs_here + (a_ref[:, here].astype(F32) - theirs_here) * weight
            if form == "last":
                joined = joined * refs[0][:, here]
            put(here, joined.astype(BF16))
        if form != "last":
            put(slice(columns, wide), spread_stats(top + jnp.log2(total), count))

    if form == "halves":
        shapes = [jax.ShapeDtypeStruct((half, wide), BF16)] * 2
    elif form == "last":
        shapes = jax.ShapeDtypeStruct((rows, columns), BF16)
    else:
        shapes = jax.ShapeDtypeStruct((rows, wide), BF16)
    extra = () if gate is None else (gate,)
    return pl.pallas_call(
        body,
        out_shape=shapes,
        cost_estimate=cost(0, rows * wide, 6 * rows * wide),
        name="merge",
    )(mine, theirs, *extra)


def video_parts(wide):
    return VIDEO_PARTS if wide % (VIDEO_PARTS * LANES) == 0 else 1


def on_device(
    video_query,
    video_key,
    video_value,
    audio_query,
    audio_key,
    audio_value,
    cross_audio_query,
    cross_video_key,
    cross_video_value,
    cross_video_query,
    cross_audio_key,
    cross_audio_value,
    audio_frames,
    into_audio_slope,
    into_video_slope,
    timestep,
    video_gate,
    audio_gate,
    into_audio_gate,
    into_video_gate,
):
    tok_count = lax.axis_size("tok")
    head_count = lax.axis_size("head")
    tok = lax.axis_index("tok")
    samples, video_rows, video_columns = video_query.shape
    audio_rows, audio_columns = audio_query.shape[1:]
    patches = LV // FRAMES
    place = ((tok * head_count + lax.axis_index("head")) * video_rows).reshape(1)
    masks = [1 << b for b in reversed(range(tok_count.bit_length() - 1))]

    def gate_row(table, sample):
        return lax.dynamic_slice_in_dim(table, timestep[sample], 1, 0).astype(F32)

    def gate_part(row, part, parts):
        wide = row.shape[1] // tok_count
        piece = wide // parts
        return lax.dynamic_slice_in_dim(row, tok * wide + part * piece, piece, 1)

    def collect(own):
        for step, mask in enumerate(masks):
            received = swap(own, "tok", mask)
            if step < len(masks) - 1:
                own = stack_rows(own, received)
        return [own, received, swap(own, "head", 1), swap(received, "head", 1)]

    def across(blocks):
        return lax.all_to_all(blocks, "tok", split_axis=0, concat_axis=0, tiled=True)

    def self_part(members):
        entries = [(a, part, parts) for arrays, _, _, part, parts in members for a in arrays]
        bundle = pack(entries, tok_count)
        own = across(bundle)
        other = swap(own, "head", 1)
        segments = [
            (arrays[0].shape[0], width, gate_part(gate, part, parts))
            for arrays, width, gate, part, parts in members
        ]
        outs = self_attention(own, other, segments)
        return across(outs)

    results = []
    for s in range(samples):
        frames = jnp.broadcast_to(
            audio_frames[s][:, None].astype(F32), (audio_rows, LANES)
        ).astype(BF16)
        asked = collect(jnp.concatenate((cross_audio_query[s], frames), axis=1))
        kept = collect(jnp.concatenate((cross_audio_key[s], cross_audio_value[s]), axis=1))
        partial = audio_cross_local(
            asked, cross_video_key[s], cross_video_value[s], into_audio_slope, place, patches
        )
        got = [swap(partial[2], "head", 1), swap(partial[3], "head", 1)]
        mine = merge(partial[0], got[0], "whole")
        send = merge(partial[1], got[1], "whole")
        for step, mask in enumerate(reversed(masks)):
            received = swap(send, "tok", mask)
            if step < len(masks) - 1:
                mine, send = merge(mine, received, "halves")
            else:
                audio_cross = merge(mine, received, "last", gate_row(into_audio_gate, s))
        video = ((video_key[s], video_value[s], video_query[s]), DHV, gate_row(video_gate, s))
        audio = ((audio_key[s], audio_value[s], audio_query[s]), DHA, gate_row(audio_gate, s))
        parts = video_parts(video_columns // tok_count)
        if video_columns // parts == audio_columns:
            outs = [self_part([video + (0, parts), audio + (0, 1)])]
            sound = (outs[0], video_rows)
        else:
            outs = [self_part([video + (0, parts)])]
            sound = (self_part([audio + (0, 1)]), 0)
        for p in range(1, parts):
            outs.append(self_part([video + (p, parts)]))
        video_self, audio_self = unpack(
            [[(array, 0) for array in outs], [sound]], [video_rows, audio_rows]
        )
        video_cross = video_cross_local(
            cross_video_query[s],
            kept,
            asked,
            into_video_slope,
            gate_row(into_video_gate, s),
            place,
            patches,
        )
        results.append((video_self, audio_self, audio_cross, video_cross))
    return tuple(jnp.stack(parts) for parts in zip(*results))


def solution(mesh):
    rows = P("groups", ("tok", "head"), None)
    placed = (rows,) * 12 + (
        P("groups", ("tok", "head")),
        P(),
        P(),
        P("groups"),
        P(),
        P(),
        P(),
        P(),
    )

    return jax.shard_map(
        on_device, mesh=mesh, in_specs=placed, out_specs=(rows,) * 4, check_vma=False
    )
```

```python
import math

import jax
import jax.numpy as jnp
from jax import lax
from jax.experimental import pallas as pl
from jax.experimental.pallas import tpu as pltpu
from jax.sharding import PartitionSpec as P


LV = 4096
FRAMES = 16
DHV = 128
DHA = 64
LANES = 128
LOG2E = 1.4426950408889634
VIDEO_PARTS = 2
WIDE = 512


BF16 = jnp.bfloat16
F32 = jnp.float32


def swap(value, axis, mask):
    count = lax.axis_size(axis)
    return lax.ppermute(value, axis, [(j, j ^ mask) for j in range(count)])


def cost(flops, exps, moved):
    return pl.CostEstimate(flops=int(flops), transcendentals=int(exps), bytes_accessed=int(moved))


def nt(a, b):
    return lax.dot_general(a, b, (((1,), (1,)), ((), ())), preferred_element_type=F32)


def pack(entries, tok_count):
    rows = [a.shape[0] for a, _, _ in entries]
    wide = entries[0][0].shape[1] // tok_count // entries[0][2]
    n = len(entries)
    if wide % LANES:
        cut = [
            a.reshape(a.shape[0], tok_count, parts, wide)[:, :, part].transpose(1, 0, 2)
            for a, part, parts in entries
        ]
        return jnp.concatenate(cut, axis=1)

    def body(*refs):
        at = 0
        for a in range(n):
            refs[n][0, at : at + rows[a], :] = refs[a][...]
            at += rows[a]

    total = sum(rows)
    return pl.pallas_call(
        body,
        grid=(tok_count,),
        out_shape=jax.ShapeDtypeStruct((tok_count, total, wide), BF16),
        in_specs=[
            pl.BlockSpec((a.shape[0], wide), lambda m, p=part, q=parts: (0, m * q + p))
            for a, part, parts in entries
        ],
        out_specs=pl.BlockSpec((1, total, wide), lambda m: (m, 0, 0)),
        cost_estimate=cost(0, 0, 4 * total * tok_count * wide),
        name="pack",
    )(*[a for a, _, _ in entries])


def unpack(sources, rows):
    tok_count = sources[0][0][0].shape[0]
    wides = [entry[0][0].shape[2] for entry in sources]
    parts = [len(entry) for entry in sources]
    if any(w % LANES for w in wides):
        outs = []
        for entry, r, w in zip(sources, rows, wides):
            cut = [array[:, at : at + r].transpose(1, 0, 2) for array, at in entry]
            outs.append(jnp.stack(cut, axis=2).reshape(r, tok_count * len(entry) * w))
        return outs

    each = math.gcd(tok_count, 2)

    def body(*refs):
        at = 0
        for e, (w, count) in enumerate(zip(wides, parts)):
            out = refs[sum(parts) + e]
            for p in range(count):
                for m in range(each):
                    here = (m * count + p) * w
                    out[:, here : here + w] = refs[at][m]
                at += 1

    flat = [(array, at, r) for entry, r in zip(sources, rows) for array, at in entry]
    for _, at, r in flat:
        assert at % r == 0
    return pl.pallas_call(
        body,
        grid=(tok_count // each,),
        out_shape=[
            jax.ShapeDtypeStruct((r, tok_count * w * count), BF16)
            for r, w, count in zip(rows, wides, parts)
        ],
        in_specs=[
            pl.BlockSpec((each, r, array.shape[2]), lambda m, k=at // r: (m, k, 0))
            for array, at, r in flat
        ],
        out_specs=[
            pl.BlockSpec((r, each * w * count), lambda m: (0, m))
            for r, w, count in zip(rows, wides, parts)
        ],
        cost_estimate=cost(0, 0, 4 * sum(r * w for r, w in zip(rows, wides)) * tok_count),
        name="unpack",
    )(*[array for array, _, _ in flat])


def stack_rows(*arrays):
    rows, wide = arrays[0].shape
    count = len(arrays)

    def body(*refs):
        for m in range(count):
            refs[count][m * rows : (m + 1) * rows] = refs[m][...]

    return pl.pallas_call(
        body,
        out_shape=jax.ShapeDtypeStruct((count * rows, wide), BF16),
        cost_estimate=cost(0, 0, 4 * count * rows * wide),
        name="stack_rows",
    )(*arrays)


def lane_of(shape):
    return lax.broadcasted_iota(jnp.int32, shape, len(shape) - 1)


def one_head(queries, parts, scale):
    factor = scale * LOG2E
    top = total = summed = None
    for keys, values in parts:
        scores = nt(queries, keys)
        peak = jnp.max(scores, axis=1, keepdims=True)
        new_top = peak if top is None else jnp.maximum(top, peak)
        exps = jnp.exp2((scores - new_top) * factor)
        sums = jnp.sum(exps, axis=1, keepdims=True)
        part = jnp.dot(exps.astype(BF16), values, preferred_element_type=F32)
        if top is None:
            total, summed = sums, part
        else:
            fade = jnp.exp2((top - new_top) * factor)
            total = total * fade + sums
            summed = summed * fade + part
        top = new_top
    return total, summed


def pick(lanes, width, keys, index):
    if lanes == width:
        return keys
    here = (lane_of(keys.shape) // width) == index
    return jnp.where(here, keys, jnp.zeros_like(keys))


def self_attention(own, other, segments):
    tok_count, total, columns = own.shape
    lanes = min(LANES, columns)

    def body(*refs):
        out_ref = refs[-1]
        row_at = 0
        for g, (rows, width, _) in enumerate(segments):
            key_a, value_a, q_ref, key_b, value_b, gate_ref = refs[6 * g : 6 * g + 6]
            gates = gate_ref[...]
            heads = lanes // width
            scale = 1.0 / math.sqrt(width)
            some = max(1, min(tok_count, 512 // rows))
            span = max(1, min(tok_count, 1024 // rows))
            here = slice(row_at, row_at + rows)
            row_at += rows

            def step(b, carry):
                at = b * some
                q = q_ref[pl.ds(at, some)].reshape(some * rows, lanes)
                result = None
                for head in range(heads):
                    parts = []
                    for keys, values in ((key_a, value_a), (key_b, value_b)):
                        for c in range(0, tok_count, span):
                            k = keys[c : c + span].reshape(span * rows, lanes)
                            v = values[c : c + span].reshape(span * rows, lanes)
                            parts.append((pick(lanes, width, k, head), v))
                    whole, summed = one_head(q, parts, scale)
                    done = summed / whole
                    if result is None:
                        result = done
                    else:
                        result = jnp.where(lane_of(done.shape) // width == head, done, result)
                result = (result * gates).astype(BF16)
                out_ref[pl.ds(at, some), here, :] = result.reshape(some, rows, lanes)
                return carry

            lax.fori_loop(0, tok_count // some, step, 0)

    in_specs, operands = [], []
    scores = base = 0
    for rows, width, gate in segments:
        assert base % rows == 0
        first = base // rows
        for array, which in ((own, 0), (own, 1), (own, 2), (other, 0), (other, 1)):
            in_specs.append(
                pl.BlockSpec((tok_count, rows, lanes), lambda i, k=first + which: (0, k, i))
            )
            operands.append(array)
        in_specs.append(pl.BlockSpec((1, lanes), lambda i: (0, i)))
        operands.append(gate)
        scores += (tok_count * rows) ** 2 * 2 * (columns // width)
        base += 3 * rows
    out_rows = sum(rows for rows, _, _ in segments)
    return pl.pallas_call(
        body,
        grid=(columns // lanes,),
        out_shape=jax.ShapeDtypeStruct((tok_count, out_rows, columns), BF16),
        in_specs=in_specs,
        out_specs=pl.BlockSpec((tok_count, out_rows, lanes), lambda i: (0, 0, i)),
        cost_estimate=cost(scores * 4 * LANES, scores, 10 * tok_count * total * columns),
        name="self_attention",
    )(*operands)


def video_cross_local(queries, pieces, marks, slopes, gate, place, span):
    counted, columns = queries.shape
    keyed = pieces[0].shape[0]
    n = len(pieces)
    block = WIDE if columns % WIDE == 0 else LANES
    steps = columns // block
    heads = LANES // DHA
    factor = LOG2E / math.sqrt(DHA)

    def body(slope_ref, place_ref, q_ref, *refs):
        gate_ref, out_ref = refs[3 * n :]
        i = pl.program_id(0)
        at = place_ref[0]
        if span % counted == 0:
            mine = (at // span).astype(F32)
        else:
            col = lax.broadcasted_iota(jnp.int32, (1, counted), 1)
            mine = ((at + col) // span).astype(F32)
        gaps = []
        for p in range(n):
            frame = refs[3 * p + 2][...].astype(F32)
            if span % counted != 0 and counted > LANES:
                frame = jnp.concatenate([frame] * (counted // LANES), axis=1)
            if counted < LANES:
                frame = frame[:, :counted]
            gaps.append(jnp.abs(frame - mine))
        for j in range(block // LANES):
            here = slice(j * LANES, (j + 1) * LANES)
            q = q_ref[:, here]
            turned = [jnp.transpose(refs[3 * p + 1][:, here]) for p in range(n)]
            results = []
            for head in range(heads):
                slope = slope_ref[(i * (block // LANES) + j) * heads + head] * LOG2E
                scores = []
                for p in range(n):
                    bias = gaps[p] * slope
                    if bias.shape[1] < counted:
                        bias = jnp.concatenate([bias] * (counted // LANES), axis=1)
                    keys = pick(LANES, DHA, refs[3 * p][:, here], head)
                    scores.append(nt(keys, q) * factor - bias)
                top = jnp.max(scores[0], axis=0, keepdims=True)
                for one in scores[1:]:
                    top = jnp.maximum(top, jnp.max(one, axis=0, keepdims=True))
                total = summed = None
                for p in range(n):
                    exps = jnp.exp2(scores[p] - top)
                    sums = jnp.sum(exps, axis=0, keepdims=True)
                    part = jnp.dot(
                        turned[p][head * DHA : (head + 1) * DHA],
                        exps.astype(BF16),
                        preferred_element_type=F32,
                    )
                    total = sums if total is None else total + sums
                    summed = part if summed is None else summed + part
                results.append(summed * (1.0 / total))
            result = jnp.transpose(jnp.concatenate(results, axis=0))
            out_ref[:, here] = (result * gate_ref[:, here]).astype(BF16)

    each = marks[0].shape[0] // keyed
    pairs = [pl.BlockSpec((keyed, block), lambda i, k=k: (0, k * steps + i)) for k in (0, 1)]
    specs, operands = [], []
    for p in range(n):
        specs += pairs
        specs.append(
            pl.BlockSpec((keyed, LANES), lambda i, r=p % each: (r, columns // LANES))
        )
        operands += [pieces[p], pieces[p], marks[p // each]]
    scores = counted * keyed * n * columns // DHA
    return pl.pallas_call(
        body,
        grid=(steps,),
        out_shape=jax.ShapeDtypeStruct((counted, columns), BF16),
        in_specs=[
            pl.BlockSpec(memory_space=pltpu.SMEM),
            pl.BlockSpec(memory_space=pltpu.SMEM),
            pl.BlockSpec((counted, block), lambda i: (0, i)),
        ]
        + specs
        + [pl.BlockSpec((1, block), lambda i: (0, i))],
        out_specs=pl.BlockSpec((counted, block), lambda i: (0, i)),
        cost_estimate=cost(scores * 4 * LANES, scores, 4 * columns * (counted + n * keyed)),
        name="video_cross",
    )(slopes, place, queries, *operands, gate)


def audio_cross_local(pieces, keys, values, slopes, place, span):
    counted = pieces[0].shape[0]
    n = len(pieces)
    keyed, columns = keys.shape
    steps = columns // LANES
    heads = LANES // DHA
    count = steps * heads
    factor = LOG2E / math.sqrt(DHA)

    def body(slope_ref, place_ref, k_ref, v_ref, *refs):
        q_refs, f_refs, o_refs = refs[:n], refs[n : 2 * n], refs[2 * n : 3 * n]
        stats, times = refs[3 * n :]
        i = pl.program_id(0)
        at = place_ref[0]

        @pl.when(i == 0)
        def _():
            stats[...] = jnp.zeros_like(stats)
            for p in range(n):
                here = slice(p * counted, (p + 1) * counted)
                times[:, here] = jnp.transpose(f_refs[p][...].astype(F32))[0:8, :]

        @pl.when(i < steps)
        def _():
            keys_here = k_ref[...]
            turned = jnp.transpose(v_ref[...])
            q = jnp.concatenate([r[...] for r in q_refs], axis=0)
            mine = times[0:1, :]
            if span % keyed == 0:
                gap = jnp.abs(mine - (at // span).astype(F32))
            else:
                row = lax.broadcasted_iota(jnp.int32, (keyed, 1), 0)
                gap = jnp.abs(mine - ((at + row) // span).astype(F32))
            results = []
            for head in range(heads):
                index = i * heads + head
                slope = slope_ref[index] * LOG2E
                scores = nt(pick(LANES, DHA, keys_here, head), q)
                if span % keyed == 0:
                    top = jnp.max(scores, axis=0, keepdims=True)
                    exps = jnp.exp2((scores - top) * factor)
                    top = top * factor - gap * slope
                else:
                    scores = scores * factor - gap * slope
                    top = jnp.max(scores, axis=0, keepdims=True)
                    exps = jnp.exp2(scores - top)
                total = jnp.sum(exps, axis=0, keepdims=True)
                part = jnp.dot(
                    turned[head * DHA : (head + 1) * DHA],
                    exps.astype(BF16),
                    preferred_element_type=F32,
                )
                results.append(part * (1.0 / total))
                stats[pl.ds(index, 1), :] = top + jnp.log2(total)
            result = jnp.transpose(jnp.concatenate(results, axis=0).astype(BF16))
            for p in range(n):
                o_refs[p][...] = result[p * counted : (p + 1) * counted]

        @pl.when(i == steps)
        def _():
            for p in range(n):
                here = slice(p * counted, (p + 1) * counted)
                o_refs[p][...] = spread_stats(jnp.transpose(stats[:, here]), count)

    def at_step(i):
        return jnp.minimum(i, steps - 1)

    scores = counted * keyed * n * count
    return pl.pallas_call(
        body,
        grid=(steps + 1,),
        out_shape=[jax.ShapeDtypeStruct((counted, columns + LANES), BF16)] * n,
        in_specs=[
            pl.BlockSpec(memory_space=pltpu.SMEM),
            pl.BlockSpec(memory_space=pltpu.SMEM),
        ]
        + [pl.BlockSpec((keyed, LANES), lambda i: (0, at_step(i)))] * 2
        + [pl.BlockSpec((counted, LANES), lambda i: (0, at_step(i)))] * n
        + [pl.BlockSpec((counted, LANES), lambda i: (0, steps))] * n,
        out_specs=[pl.BlockSpec((counted, LANES), lambda i: (0, i))] * n,
        scratch_shapes=[
            pltpu.VMEM((LANES, n * counted), F32),
            pltpu.VMEM((8, n * counted), F32),
        ],
        cost_estimate=cost(scores * 4 * LANES, scores, 4 * columns * (n * counted + keyed)),
        name="audio_cross",
    )(slopes, place, keys, values, *pieces, *pieces)


def spread_stats(stats, count):
    lane = lane_of(stats.shape)
    first = stats.astype(BF16).astype(F32)
    rest = stats - first
    second = rest.astype(BF16).astype(F32)
    third = rest - second
    second = pltpu.roll(second, count, 1)
    third = pltpu.roll(third, 2 * count, 1)
    packed = jnp.where(lane < count, first, jnp.where(lane < 2 * count, second, third))
    return jnp.where(lane < 3 * count, packed, 0.0).astype(BF16)


def read_stats(packed, count):
    terms = packed.astype(F32)
    second = pltpu.roll(terms, LANES - count, 1)
    third = pltpu.roll(terms, LANES - 2 * count, 1)
    return terms + second + third


def merge(mine, theirs, form, gate=None):
    rows, wide = mine.shape
    columns = wide - LANES
    count = columns // DHA
    heads = LANES // DHA
    half = rows // 2

    def body(a_ref, b_ref, *refs):
        a_stat = read_stats(a_ref[:, columns:], count)
        b_stat = read_stats(b_ref[:, columns:], count)
        top = jnp.maximum(a_stat, b_stat)
        a_part = jnp.exp2(a_stat - top)
        total = a_part + jnp.exp2(b_stat - top)
        share = a_part / total
        high = share.astype(BF16)
        low = (share - high.astype(F32)).astype(BF16)

        def put(here, value):
            if form == "halves":
                refs[0][:, here] = value[:half]
                refs[1][:, here] = value[half:]
            else:
                refs[-1][:, here] = value

        for j in range(columns // LANES):
            here = slice(j * LANES, (j + 1) * LANES)
            row = lax.broadcasted_iota(jnp.int32, (LANES, LANES), 0)
            spot = (row == j * heads + lane_of((LANES, LANES)) // DHA).astype(F32).astype(BF16)
            weight = jnp.dot(high, spot, preferred_element_type=F32)
            weight = weight + jnp.dot(low, spot, preferred_element_type=F32)
            theirs_here = b_ref[:, here].astype(F32)
            joined = theirs_here + (a_ref[:, here].astype(F32) - theirs_here) * weight
            if form == "last":
                joined = joined * refs[0][:, here]
            put(here, joined.astype(BF16))
        if form != "last":
            put(slice(columns, wide), spread_stats(top + jnp.log2(total), count))

    if form == "halves":
        shapes = [jax.ShapeDtypeStruct((half, wide), BF16)] * 2
    else:
        shapes = jax.ShapeDtypeStruct((rows, columns), BF16)
    extra = () if gate is None else (gate,)
    return pl.pallas_call(
        body,
        out_shape=shapes,
        cost_estimate=cost(0, rows * wide, 6 * rows * wide),
        name="merge",
    )(mine, theirs, *extra)


def video_parts(wide):
    return VIDEO_PARTS if wide % (VIDEO_PARTS * LANES) == 0 else 1


def on_device(
    video_query,
    video_key,
    video_value,
    audio_query,
    audio_key,
    audio_value,
    cross_audio_query,
    cross_video_key,
    cross_video_value,
    cross_video_query,
    cross_audio_key,
    cross_audio_value,
    audio_frames,
    into_audio_slope,
    into_video_slope,
    timestep,
    video_gate,
    audio_gate,
    into_audio_gate,
    into_video_gate,
):
    tok_count = lax.axis_size("tok")
    head_count = lax.axis_size("head")
    tok = lax.axis_index("tok")
    samples, video_rows, video_columns = video_query.shape
    audio_rows, audio_columns = audio_query.shape[1:]
    patches = LV // FRAMES
    place = ((tok * head_count + lax.axis_index("head")) * video_rows).reshape(1)
    masks = [1 << b for b in reversed(range(tok_count.bit_length() - 1))]

    def gate_row(table, sample):
        return lax.dynamic_slice_in_dim(table, timestep[sample], 1, 0).astype(F32)

    def gate_part(row, part, parts):
        wide = row.shape[1] // tok_count
        piece = wide // parts
        return lax.dynamic_slice_in_dim(row, tok * wide + part * piece, piece, 1)

    def collect(own):
        for step, mask in enumerate(masks):
            received = swap(own, "tok", mask)
            if step < len(masks) - 1:
                own = stack_rows(own, received)
        return [own, received, swap(own, "head", 1), swap(received, "head", 1)]

    def collect_soon(own):
        for mask in masks[:-2]:
            received = swap(own, "tok", mask)
            own = stack_rows(own, received)
        ends = masks[-2:] + ([3] if len(masks) > 1 else [])
        received = [swap(own, "tok", mask) for mask in ends]
        own = stack_rows(own, *received)
        return [own, swap(own, "head", 1)]

    def across(blocks):
        return lax.all_to_all(blocks, "tok", split_axis=0, concat_axis=0, tiled=True)

    def self_part(members):
        entries = [(a, part, parts) for arrays, _, _, part, parts in members for a in arrays]
        bundle = pack(entries, tok_count)
        own = across(bundle)
        other = swap(own, "head", 1)
        segments = [
            (arrays[0].shape[0], width, gate_part(gate, part, parts))
            for arrays, width, gate, part, parts in members
        ]
        outs = self_attention(own, other, segments)
        return across(outs)

    results = []
    for s in range(samples):
        frames = jnp.broadcast_to(
            audio_frames[s][:, None].astype(F32), (audio_rows, LANES)
        ).astype(BF16)
        asked = collect_soon(jnp.concatenate((cross_audio_query[s], frames), axis=1))
        kept = collect(jnp.concatenate((cross_audio_key[s], cross_audio_value[s]), axis=1))
        partial = audio_cross_local(
            asked, cross_video_key[s], cross_video_value[s], into_audio_slope, place, patches
        )
        received = swap(partial[1], "head", 1)
        mine, send = merge(partial[0], received, "halves")
        for step, mask in enumerate(reversed(masks)):
            received = swap(send, "tok", mask)
            if step < len(masks) - 1:
                mine, send = merge(mine, received, "halves")
            else:
                audio_cross = merge(mine, received, "last", gate_row(into_audio_gate, s))
        video = ((video_key[s], video_value[s], video_query[s]), DHV, gate_row(video_gate, s))
        audio = ((audio_key[s], audio_value[s], audio_query[s]), DHA, gate_row(audio_gate, s))
        parts = video_parts(video_columns // tok_count)
        if video_columns // parts == audio_columns:
            outs = [self_part([video + (0, parts), audio + (0, 1)])]
            sound = (outs[0], video_rows)
        else:
            outs = [self_part([video + (0, parts)])]
            sound = (self_part([audio + (0, 1)]), 0)
        for p in range(1, parts):
            outs.append(self_part([video + (p, parts)]))
        video_self, audio_self = unpack(
            [[(array, 0) for array in outs], [sound]], [video_rows, audio_rows]
        )
        video_cross = video_cross_local(
            cross_video_query[s],
            kept,
            asked,
            into_video_slope,
            gate_row(into_video_gate, s),
            place,
            patches,
        )
        results.append((video_self, audio_self, audio_cross, video_cross))
    return tuple(jnp.stack(parts) for parts in zip(*results))


def solution(mesh):
    rows = P("groups", ("tok", "head"), None)
    placed = (rows,) * 12 + (
        P("groups", ("tok", "head")),
        P(),
        P(),
        P("groups"),
        P(),
        P(),
        P(),
        P(),
    )

    return jax.shard_map(
        on_device, mesh=mesh, in_specs=placed, out_specs=(rows,) * 4, check_vma=False
    )
```
